32 devices in a mesh: gx: 8 (over y, x, core), gy: 4 (over z).
Axes of the slice: x: 2, y: 2, z: 4, core: 2. Of those that a mesh axis runs over, the one named last changes fastest.
Arguments:
- pressure: float32 [128, 256, 512], P('gx', 'gy'), may hold values from -3 to 3
- permeability: float32 [128, 256, 512], P('gx', 'gy'), may hold values from 0.1 to 1
- kernel: float32 [2, 1536, 1536], P(None, 'gx', 'gy'), may hold values from -1.2247449 to 1.2247449
- slip_rate: float32 [1536], P(('gx', 'gy')), may hold values from 0.1 to 1
- aging_state: float32 [1536], P(('gx', 'gy')), may hold values from 0.5 to 5
- normal_stress: float32 [1536], P(('gx', 'gy')), may hold values from 50 to 80
- shear_stress: float32 [1536], P(('gx', 'gy')), may hold values from 33 to 45
- direct_effect: float32 [1536], P(('gx', 'gy')), may hold values from 0.01 to 0.02
- evolution_effect: float32 [1536], P(('gx', 'gy')), may hold values from 0.01 to 0.03
- slip_distance: float32 [1536], P(('gx', 'gy')), may hold values from 0.2 to 1
- tri_owner: int32 [1536, 1], P(('gx', 'gy')), may hold values from 0 to 7; in each aligned block of 48 rows (0 to 47, 48 to 95, ...) at most 12 rows name the same one
- tri_cell: int32 [1536], P(('gx', 'gy')), may hold values from 0 to 524287
Outputs:
- pressure_next: float32 [128, 256, 512], P('gx', 'gy')
- state_next: float32 [1536], P(('gx', 'gy'))
- log_rate: float32 [1536], P(('gx', 'gy'))
The draws below stay inside these ranges and needn't reach their ends.
Inputs may be any that keep to these rules, and one draw needn't show every extreme that they name: `tri_owner`: at most 12 of the 48 triangles of one device name one owner, and in every draw some owner is named by exactly 12 triangles of some device.
All inputs are finite; a program needn't handle non-finite values.
Results may differ from the reference program's by a relative error of at most 0.000092.
Values sent between devices are 32-bit elements; how exact they have to be, the bound alone decides.
A program may use at most 64 MiB of HBM per device.

```python
import math
import jax
import jax.numpy as jnp
import numpy as np
from jax import lax

CX = 16
CY = 64
NZ = 512
SWEEPS = 3
TRI_DEV = 48
NTRI = 1536
CAP = 12
NX = 128
NY = 256
N_GX = 8
N_GY = 4


def set_ends(values, key, least, top_value):
    spot = [jax.random.randint(jax.random.fold_in(key, axis), (), 0, length) for axis, length in enumerate(values.shape)]
    main_axis = values.shape.index(max(values.shape))
    beside = spot[:main_axis] + [(spot[main_axis] + 1) % values.shape[main_axis]] + spot[main_axis + 1:]
    return values.at[tuple(spot)].set(least).at[tuple(beside)].set(top_value)


def level_of(rng, dims, pieces, smallest, top_value):
    def one(position, shards_of):
        heights = jax.random.uniform(jax.random.fold_in(jax.random.fold_in(rng, 6), position), (shards_of,), jnp.float32, smallest / len(pieces), top_value / len(pieces))
        return jnp.repeat(jnp.exp(heights), dims[position] // shards_of).reshape((-1,) + (1,) * (len(dims) - position - 1))

    level = one(*pieces[0])
    for cut in pieces[1:]:
        level = level * one(*cut)
    return level


def routed_block(rng, own, number, rows, amount, top, limit, skew):
    sequence = jax.random.permutation(rng, amount)
    packed, common = shares(amount, rows * top, limit, skew, True), shares(amount, rows * top, limit, skew, False)
    places = jnp.arange(amount)

    def named(lengths, offset_by):
        used = int((lengths > 0).sum())
        fixed = max(1, used // 4)
        passed = fixed + (places - fixed + offset_by * (used - fixed)) % max(1, amount - fixed)
        return jnp.zeros((amount,), jnp.int32).at[sequence[jnp.where(places < fixed, places, passed)]].set(jnp.asarray(lengths, jnp.int32))

    lengths = jnp.where(number % 4 == 0, named(packed, number // 4), named(common, number - number // 4 - 1))
    mixed = jax.random.permutation(jax.random.fold_in(own, 3), amount)
    source_of, receiver = mixed[0:amount // 2 * 2:2], mixed[1:amount // 2 * 2:2]
    slack = jnp.minimum(lengths[source_of] - 1, limit - lengths[receiver]) // 2
    slack = jnp.where((source_of == sequence[0]) | (receiver == sequence[0]) | (lengths[receiver] == 0), 0, jnp.maximum(slack, 0))
    passed = jax.random.randint(jax.random.fold_in(own, 4), (amount // 2,), 0, 1 << 20) % (slack + 1)
    lengths = lengths.at[source_of].add(-passed).at[receiver].add(passed)
    labels = jnp.searchsorted(jnp.cumsum(lengths), jnp.arange(rows * top), side="right").astype(jnp.int32)
    table = labels.reshape(top, rows).T
    table = table[jax.random.permutation(jax.random.fold_in(own, 1), rows)]
    offset_by = jax.random.randint(jax.random.fold_in(own, 2), (rows, 1), 0, top)
    return jnp.take_along_axis(table, (jnp.arange(top)[None, :] + offset_by) % top, axis=1)


def shares(count, total, bound, skew, full):
    loads = [(1 << 20) // math.isqrt(grade ** skew) + 1 for grade in range(1, count + 1)]
    largest = bound if full else min(bound, max(-(-total // count), total * loads[0] // sum(loads)))
    least = 1 if total - largest >= count - 1 else 0
    counts, spare = [largest] + [least] * (count - 1), total - largest - least * (count - 1)
    while spare > 0:
        candidates = [i for i in range(1, count) if counts[i] < largest] or [i for i in range(1, count) if counts[i] < bound]
        whole, left = sum([loads[i] for i in candidates]), spare
        for i in candidates:
            more = min(bound - counts[i], max(1, left * loads[i] // whole), spare)
            counts[i] = counts[i] + more
            spare = spare - more
    return np.array(counts)


def scatter_about(rng, shape, spread, most, pieces=(), held_as=jnp.bfloat16):
    array = spread * jax.random.normal(rng, shape, jnp.float32)
    if pieces:
        array = array * level_of(rng, shape, pieces, -0.22, 0.18)
    return jnp.clip(array, -most, most).astype(held_as)


def setup_inputs(seed: int = 0) -> dict:
    splits = jax.random.split(jax.random.key(seed), 13)
    pressure = scatter_about(splits[0], (NX, NY, NZ), 1.0, 3.0, ((0, 8), (1, 4)), jnp.float32)
    permeability = jnp.clip(jnp.exp(math.log(1.0) - 2.3025851 * jax.random.uniform(splits[1], (NX, NY, NZ), jnp.float32) ** level_of(splits[1], (NX, NY, NZ), ((0, 8), (1, 4)), -0.2, 0.2)), 0.1, 1.0)
    kernel = scatter_about(splits[2], (2, NTRI, NTRI), (8.0 / NTRI ** 0.5), 1.2247449, ((1, 8), (2, 4)), jnp.float32)
    slip_rate = jnp.clip(jnp.exp(math.log(1.0) - 2.3025851 * jax.random.uniform(splits[3], (NTRI,), jnp.float32) ** level_of(splits[3], (NTRI,), ((0, 32),), -0.2, 0.2)), 0.1, 1.0)
    aging_state = jnp.clip(jnp.exp(math.log(5.0) - 2.3025851 * jax.random.uniform(splits[4], (NTRI,), jnp.float32) ** level_of(splits[4], (NTRI,), ((0, 32),), -0.2, 0.2)), 0.5, 5.0)
    normal_stress = jnp.clip(50.0 + 30.0 * jax.random.uniform(splits[5], (NTRI,), jnp.float32) ** level_of(splits[5], (NTRI,), ((0, 32),), -0.2, 0.2), 50.0, 80.0)
    shear_stress = jnp.clip(33.0 + 12.0 * jax.random.uniform(splits[6], (NTRI,), jnp.float32) ** level_of(splits[6], (NTRI,), ((0, 32),), -0.2, 0.2), 33.0, 45.0)
    direct_effect = jnp.clip(jnp.exp(math.log(0.02) - 0.6931472 * jax.random.uniform(splits[7], (NTRI,), jnp.float32) ** level_of(splits[7], (NTRI,), ((0, 32),), -0.2, 0.2)), 0.01, 0.02)
    evolution_effect = jnp.clip(jnp.exp(math.log(0.03) - 1.0986123 * jax.random.uniform(splits[8], (NTRI,), jnp.float32) ** level_of(splits[8], (NTRI,), ((0, 32),), -0.2, 0.2)), 0.01, 0.03)
    slip_distance = jnp.clip(jnp.exp(math.log(1.0) - 1.609438 * jax.random.uniform(splits[9], (NTRI,), jnp.float32) ** level_of(splits[9], (NTRI,), ((0, 32),), -0.2, 0.2)), 0.2, 1.0)
    tri_owner_keys = jax.random.split(jax.random.fold_in(splits[10], 1), NTRI // TRI_DEV)
    tri_owner_turns = jax.random.permutation(jax.random.fold_in(splits[10], 3), NTRI // TRI_DEV)
    tri_owner = jax.vmap(lambda own, number: routed_block(jax.random.fold_in(splits[10], 2), own, number, TRI_DEV, N_GX, 1, CAP, 2))(tri_owner_keys, tri_owner_turns).reshape((NTRI, 1))
    tri_cell = set_ends(jax.random.randint(splits[11], (NTRI,), 0, CX * CY * NZ), jax.random.fold_in(splits[11], 1), 0, (CX * CY * NZ) - 1).astype(jnp.int32)
    return {"pressure": pressure, "permeability": permeability, "kernel": kernel, "slip_rate": slip_rate, "aging_state": aging_state, "normal_stress": normal_stress, "shear_stress": shear_stress, "direct_effect": direct_effect, "evolution_effect": evolution_effect, "slip_distance": slip_distance, "tri_owner": tri_owner, "tri_cell": tri_cell}


conductance = 0.15
step_time = 1.0
heal_time = 0.5
friction_ref = 0.6
neighbours = ((1, 0, 0), (-1, 0, 0), (0, 1, 0), (0, -1, 0), (0, 0, 1), (0, 0, -1))

def shifted(values, step_x, step_y, step_z):
    return values[1 + step_x:values.shape[0] - 1 + step_x, 1 + step_y:values.shape[1] - 1 + step_y, 1 + step_z:values.shape[2] - 1 + step_z]

def explicit_step(padded_p, padded_k):
    full_p = jnp.pad(padded_p, ((0, 0), (0, 0), (1, 1)))
    full_k = jnp.pad(padded_k, ((0, 0), (0, 0), (1, 1)))
    centre_p = shifted(full_p, 0, 0, 0)
    centre_k = shifted(full_k, 0, 0, 0)
    flux = jnp.zeros_like(centre_p)
    for offset in neighbours:
        other_p = shifted(full_p, offset[0], offset[1], offset[2])
        other_k = shifted(full_k, offset[0], offset[1], offset[2])
        flux = flux + jnp.sqrt(centre_k * other_k) * (other_p - centre_p)
    return centre_p + conductance * flux

def reference(pressure, permeability, kernel, slip_rate, aging_state, normal_stress, shear_stress, direct_effect, evolution_effect, slip_distance, tri_owner, tri_cell):
    padded_k = jnp.pad(permeability, ((1, 1), (1, 1), (0, 0)))
    pressure_field = pressure
    for repeat in range(SWEEPS):
        pressure_field = explicit_step(jnp.pad(pressure_field, ((1, 1), (1, 1), (0, 0))), padded_k)
    triangles = jnp.arange(NTRI, dtype=jnp.int32)
    column_dev = triangles // TRI_DEV % N_GY
    owners = tri_owner[:, 0].astype(jnp.int32)
    pos_x = owners * CX + tri_cell // (CY * NZ)
    pos_y = column_dev * CY + tri_cell // NZ % CY
    pos_z = tri_cell % NZ
    fault_pressure = pressure_field[pos_x, pos_y, pos_z]
    rates = jnp.dot(kernel.reshape(2 * NTRI, NTRI), slip_rate, precision=lax.Precision.HIGHEST).reshape(2, NTRI)
    shear = shear_stress + step_time * rates[0]
    effective = normal_stress + step_time * rates[1] - fault_pressure
    ratio = slip_distance / slip_rate
    state_next = ratio + (aging_state - ratio) * jnp.exp(-heal_time / ratio)
    log_rate = (shear / effective - friction_ref - evolution_effect * jnp.log(state_next / slip_distance)) / direct_effect
    return (pressure_field, state_next, log_rate)
```

```python
import functools

import jax
import jax.numpy as jnp
from jax import lax
from jax.experimental import pallas as pl
from jax.experimental.pallas import tpu as pltpu
from jax.sharding import PartitionSpec as P

SWEEPS = 3
LANES = 128
MESH = pl.DeviceIdType.MESH

conductance = 0.15
step_time = 1.0
heal_time = 0.5
friction_ref = 0.6


def step_kernel(
    dims,
    p_hbm,
    k_hbm,
    g_hbm,
    slip_ref,
    aging_ref,
    normal_ref,
    shear_ref,
    direct_ref,
    evolution_ref,
    distance_ref,
    owner_ref,
    cell_ref,
    out_hbm,
    state_ref,
    log_ref,
    p_in,
    k_in,
    g_in,
    out_v,
    root,
    u_a,
    u_b,
    coef_a,
    coef_c,
    inv,
    first_x,
    later_x,
    first_y_send,
    first_y,
    later_y_send,
    later_y,
    slip_send,
    slip_recv,
    req_send,
    req_recv,
    req_smem,
    part_send,
    part_recv,
    ans_send,
    ans_recv,
    load_sem,
    fx_send,
    fx_recv,
    lx_send,
    lx_recv,
    y_send,
    y_recv,
    slip_ssem,
    slip_rsem,
    req_ssem,
    req_rsem,
    part_ssem,
    part_rsem,
    ans_ssem,
    ans_rsem,
):
    n_gx, n_gy, cx, cy, nz, tri, rows, cols, cap, cap_pad = dims
    nb = nz // LANES
    yp = cy + 8
    gx, gy = lax.axis_index("gx"), lax.axis_index("gy")
    dev = gx * n_gy + gy
    slip_gy = dev // n_gx
    slip_slot = dev % n_gx
    lane = lax.broadcasted_iota(jnp.int32, (1, LANES), 1)

    load_k = pltpu.make_async_copy(k_hbm, k_in, load_sem.at[0])
    load_p = pltpu.make_async_copy(p_hbm, p_in, load_sem.at[1])
    load_g = pltpu.make_async_copy(g_hbm, g_in, load_sem.at[2])
    load_k.start()
    load_p.start()
    load_g.start()

    barrier = pltpu.get_barrier_semaphore()

    def greet(x, y):
        pl.semaphore_signal(barrier, inc=1, device_id={"gx": x, "gy": y}, device_id_type=MESH)

    for off in range(1, n_gx):
        greet((gx + off) % n_gx, gy)
    for off in range(1, n_gy):
        greet(gx, (gy + off) % n_gy)
    for i in range(n_gx):
        source = gy * n_gx + i

        @pl.when(source != dev)
        def _():
            greet(source // n_gy, source % n_gy)

    zero = jnp.zeros((8, LANES), jnp.float32)
    n_col = (cx + 2) * nb
    for ref in (root, u_a, u_b):

        def clear_pad(c, _, ref=ref):
            ref[pl.ds(pl.multiple_of(c * yp, 8), 8), :] = zero
            return 0

        lax.fori_loop(0, n_col + 1, clear_pad, 0)

        def clear_end(c, _, ref=ref):
            ref[pl.ds(pl.multiple_of(c * 8, 8), 8), :] = zero
            ref[pl.ds(pl.multiple_of((cx + 1) * nb * yp + c * 8, 8), 8), :] = zero
            return 0

        lax.fori_loop(0, nb * yp // 8, clear_end, 0)

    slip_send[...] = jnp.zeros_like(slip_send)
    slip_send[0, :, :tri] = slip_ref[...]

    owner_row = owner_ref[...]
    cell_row = cell_ref[...]
    t_row = lax.broadcasted_iota(jnp.int32, (tri, tri), 1)
    t_col = lax.broadcasted_iota(jnp.int32, (tri, tri), 0)
    eye = t_row == t_col
    owner_wide = jnp.broadcast_to(owner_row, (tri, tri))
    owner_col = jnp.sum(jnp.where(eye, owner_wide, 0), axis=1, keepdims=True)
    cell_col = jnp.sum(
        jnp.where(eye, jnp.broadcast_to(cell_row, (tri, tri)), 0), axis=1, keepdims=True
    )
    same = owner_col == owner_wide
    one_below = jnp.where(same & (t_row < t_col), 1, 0)
    one_above = jnp.where(same & (t_col < t_row), 1, 0)
    rank_col = jnp.sum(one_below, axis=1, keepdims=True)
    rank_row = jnp.sum(one_above, axis=0, keepdims=True)
    slot_col = owner_col * cap + rank_col
    slot_row = owner_row * cap_pad + rank_row
    width = req_send.shape[-1]
    slot_lane = lax.broadcasted_iota(jnp.int32, (tri, width), 1)
    req_send[0] = jnp.sum(jnp.where(slot_col == slot_lane, cell_col, 0), axis=0, keepdims=True)
    req_recv[pl.ds(gx, 1)] = req_send[...]

    @pl.when(slip_gy == gy)
    def _():
        slip_recv[pl.ds(slip_slot, 1)] = slip_send[...]

    alone = jnp.where(slip_gy == gy, 1, 0)
    pl.semaphore_wait(barrier, n_gx - 1 + n_gy - 1 + n_gx - alone)

    def remote(src, dst, send, recv, x, y):
        return pltpu.make_async_remote_copy(
            src_ref=src,
            dst_ref=dst,
            send_sem=send,
            recv_sem=recv,
            device_id={"gx": x, "gy": y},
            device_id_type=MESH,
        )

    has_lo_x, has_hi_x = gx > 0, gx < n_gx - 1
    has_lo_y, has_hi_y = gy > 0, gy < n_gy - 1
    lo_x, hi_x = jnp.maximum(gx - 1, 0), jnp.minimum(gx + 1, n_gx - 1)
    lo_y, hi_y = jnp.maximum(gy - 1, 0), jnp.minimum(gy + 1, n_gy - 1)

    def first_x_copy(side, which):
        src = (k_hbm, p_hbm)[which].at[cx - 1 if side == 0 else 0]
        return remote(
            src,
            first_x.at[side, which],
            fx_send.at[side, which],
            fx_recv.at[side, which],
            hi_x if side == 0 else lo_x,
            gy,
        )

    def later_x_copy(side, turn, ref):
        plane = cx if side == 0 else 1
        src = ref.at[pl.ds(plane * nb * yp + 8, nb * yp - 8), :]
        return remote(
            src,
            later_x.at[turn, side],
            lx_send.at[turn, side],
            lx_recv.at[turn, side],
            hi_x if side == 0 else lo_x,
            gy,
        )

    def y_copy(side, turn):
        if turn == 0:
            src, dst = first_y_send.at[side], first_y.at[side]
        else:
            src, dst = later_y_send.at[turn - 1, side], later_y.at[turn - 1, side]
        return remote(
            src,
            dst,
            y_send.at[turn, side],
            y_recv.at[turn, side],
            gx,
            hi_y if side == 0 else lo_y,
        )

    send_when_x = (has_hi_x, has_lo_x)
    recv_when_x = (has_lo_x, has_hi_x)
    send_when_y = (has_hi_y, has_lo_y)
    recv_when_y = (has_lo_y, has_hi_y)

    for side in range(2):

        @pl.when(send_when_x[side])
        def _():
            first_x_copy(side, 0).start()
            first_x_copy(side, 1).start()

    def req_copy(off):
        return remote(
            req_send.at[0],
            req_recv.at[gx],
            req_ssem.at[off],
            req_rsem.at[off],
            (gx + off) % n_gx,
            gy,
        )

    def slip_copy(g):
        return remote(
            slip_send.at[0],
            slip_recv.at[slip_slot],
            slip_ssem.at[g],
            slip_rsem.at[slip_slot],
            g,
            slip_gy,
        )

    for g in range(n_gx):

        @pl.when((g != gx) | (slip_gy != gy))
        def _():
            slip_copy(g).start()

    for off in range(1, n_gx):
        req_copy(off).start()

    load_k.wait()
    load_p.wait()

    def prepare(x, _):
        for j in range(nb):
            k = k_in[x, :, j * LANES : (j + 1) * LANES]
            p = p_in[x, :, j * LANES : (j + 1) * LANES]
            r = lax.rsqrt(k)
            s = k * r
            at = pl.ds(pl.multiple_of(((x + 1) * nb + j) * yp + 8, 8), cy)
            dense = pl.ds(pl.multiple_of((x * nb + j) * cy, 8), cy)
            root[at, :] = s
            u_a[at, :] = s * p
            inv[dense, :] = r
            coef_c[dense, :] = conductance * k
        return 0

    lax.fori_loop(0, cx, prepare, 0)

    n_face = cx * nb

    def face(y):
        return pl.ds(nb * yp + 8 + y, n_face, stride=yp)

    def dense_face(y):
        return pl.ds(y, n_face, stride=cy)

    y_of = (cy - 1, 0)
    for side in range(2):
        first_y_send[side, 0] = root[face(y_of[side]), :]
        first_y_send[side, 1] = u_a[face(y_of[side]), :]
    for side in range(2):

        @pl.when(send_when_y[side])
        def _():
            y_copy(side, 0).start()

    chunk = 16

    def around(ref, x, y0):
        here, sums = [], []
        for j in range(nb):
            at = ((x + 1) * nb + j) * yp + 8 + y0
            here.append(ref[pl.ds(pl.multiple_of(at, 8), chunk), :])
        for j in range(nb):
            at = ((x + 1) * nb + j) * yp + 8 + y0
            before = here[j - 1] if j > 0 else 0.0
            after = here[j + 1] if j < nb - 1 else 0.0
            left = pltpu.roll(jnp.where(lane == LANES - 1, before, here[j]), 1, 1)
            right = pltpu.roll(jnp.where(lane == 0, after, here[j]), LANES - 1, 1)
            total = ref[pl.ds(pl.multiple_of(at + nb * yp, 8), chunk), :]
            total = total + ref[pl.ds(pl.multiple_of(at - nb * yp, 8), chunk), :]
            total = total + (ref[pl.ds(at + 1, chunk), :] + ref[pl.ds(at - 1, chunk), :])
            sums.append(total + (left + right))
        return here, sums

    def sweep(turn, src, dst):
        def plane(x, _):
            for y0 in range(0, cy, chunk):
                here, sums = around(src, x, y0)
                if turn == 0:
                    roots, root_sums = around(root, x, y0)
                for j in range(nb):
                    dense = pl.ds(pl.multiple_of((x * nb + j) * cy + y0, 8), chunk)
                    if turn == 0:
                        a = 1.0 - conductance * (roots[j] * root_sums[j])
                        coef_a[dense, :] = a
                    else:
                        a = coef_a[dense, :]
                    new = a * here[j] + coef_c[dense, :] * sums[j]
                    if turn < SWEEPS - 1:
                        at = ((x + 1) * nb + j) * yp + 8 + y0
                        dst[pl.ds(pl.multiple_of(at, 8), chunk), :] = new
                    else:
                        out_v[x, y0 : y0 + chunk, j * LANES : (j + 1) * LANES] = (
                            new * inv[dense, :]
                        )
            return 0

        lax.fori_loop(0, cx, plane, 0)

    def fix_x(turn, side, src, dst):
        x = 0 if side == 0 else cx - 1
        for j in range(nb):
            at = pl.ds(((x + 1) * nb + j) * yp + 8, cy)
            dense = pl.ds((x * nb + j) * cy, cy)
            if turn == 0:
                k = first_x[side, 0, :, j * LANES : (j + 1) * LANES]
                s = k * lax.rsqrt(k)
                halo = s * first_x[side, 1, :, j * LANES : (j + 1) * LANES]
                less = conductance * (root[at, :] * s)
                coef_a[dense, :] = coef_a[dense, :] - less
                dst[at, :] = dst[at, :] + (coef_c[dense, :] * halo - less * src[at, :])
            else:
                halo = later_x[turn - 1, side, pl.ds(j * yp, cy), :]
                if turn < SWEEPS - 1:
                    dst[at, :] = dst[at, :] + coef_c[dense, :] * halo
                else:
                    cols_j = slice(j * LANES, (j + 1) * LANES)
                    out_v[x, :, cols_j] = out_v[x, :, cols_j] + coef_c[dense, :] * inv[
                        dense, :
                    ] * halo

    def fix_y(turn, side, src, dst):
        y = 0 if side == 0 else cy - 1
        at, dense = face(y), dense_face(y)
        if turn == 0:
            s, halo = first_y[side, 0], first_y[side, 1]
            less = conductance * (root[at, :] * s)
            coef_a[dense, :] = coef_a[dense, :] - less
            dst[at, :] = dst[at, :] + (coef_c[dense, :] * halo - less * src[at, :])
        else:
            halo = later_y[turn - 1, side]
            if turn < SWEEPS - 1:
                dst[at, :] = dst[at, :] + coef_c[dense, :] * halo
            else:
                later_y[turn - 1, side] = coef_c[dense, :] * inv[dense, :] * halo
                for x in range(cx):
                    for j in range(nb):
                        cols_j = slice(j * LANES, (j + 1) * LANES)
                        row = x * nb + j
                        out_v[x, y : y + 1, cols_j] = (
                            out_v[x, y : y + 1, cols_j] + later_y[turn - 1, side, row : row + 1, :]
                        )

    def take_halos(turn, src, dst):
        for side in range(2):

            @pl.when(recv_when_y[side])
            def _():
                y_copy(side, turn).wait_recv()
                fix_y(turn, side, src, dst)

        for side in range(2):

            @pl.when(recv_when_x[side])
            def _():
                if turn == 0:
                    first_x_copy(side, 0).wait_recv()
                    first_x_copy(side, 1).wait_recv()
                else:
                    later_x_copy(side, turn - 1, src).wait_recv()
                fix_x(turn, side, src, dst)

    def send_halos(turn, ref):
        for side in range(2):
            later_y_send[turn - 1, side] = ref[face(y_of[side]), :]
        for side in range(2):

            @pl.when(send_when_x[side])
            def _():
                later_x_copy(side, turn - 1, ref).start()

        for side in range(2):

            @pl.when(send_when_y[side])
            def _():
                y_copy(side, turn).start()

    sweep(0, u_a, u_b)
    take_halos(0, u_a, u_b)
    send_halos(1, u_b)

    for i in range(n_gx):

        @pl.when(gy * n_gx + i != dev)
        def _():
            remote(
                slip_send.at[0], slip_recv.at[i], slip_ssem.at[0], slip_rsem.at[i], gx, gy
            ).wait_recv()

    n_cb = cols // LANES
    segment = [jnp.zeros((1, LANES), jnp.float32) for _ in range(n_cb)]
    for i in range(n_gx):
        first, shift = (i * tri) // LANES, (i * tri) % LANES
        row = slip_recv[i]
        if shift:
            row = pltpu.roll(row, shift, 1)
        segment[first] = segment[first] + jnp.where(lane >= shift, row, 0.0)
        if shift + tri > LANES:
            segment[first + 1] = segment[first + 1] + jnp.where(lane < shift, row, 0.0)
    eye_f = lax.broadcasted_iota(jnp.int32, (tri, LANES), 0) == lax.broadcasted_iota(
        jnp.int32, (tri, LANES), 1
    )
    for part in range(n_gy):
        for comp in range(2):
            total = jnp.zeros((tri, LANES), jnp.float32)
            for b in range(n_cb):
                block = g_tile(g_in, load_g, part, comp, b, tri)
                total = total + block * segment[b]
            sums = jnp.sum(total, axis=1, keepdims=True)
            part_send[part, comp : comp + 1, :] = jnp.sum(
                jnp.where(eye_f, sums, 0.0), axis=0, keepdims=True
            )

    def part_copy(off):
        to = (gy + off) % n_gy
        return remote(
            part_send.at[to], part_recv.at[gy], part_ssem.at[off], part_rsem.at[off], gx, to
        )

    part_recv[pl.ds(gy, 1)] = part_send[pl.ds(gy, 1)]
    for off in range(1, n_gy):
        part_copy(off).start()

    sweep(1, u_b, u_a)
    take_halos(1, u_b, u_a)
    send_halos(2, u_a)
    for off in range(1, n_gx):
        remote(
            req_send.at[0],
            req_recv.at[(gx + n_gx - off) % n_gx],
            req_ssem.at[off],
            req_rsem.at[off],
            gx,
            gy,
        ).wait_recv()
    to_smem = pltpu.make_async_copy(req_recv, req_smem, load_sem.at[3])
    to_smem.start()
    ans_send[...] = jnp.zeros_like(ans_send)
    sweep(2, u_a, None)

    for off in range(1, n_gy):
        remote(
            part_send.at[0],
            part_recv.at[(gy + n_gy - off) % n_gy],
            part_ssem.at[off],
            part_rsem.at[off],
            gx,
            gy,
        ).wait_recv()
    rates = part_recv[0]
    for other in range(1, n_gy):
        rates = rates + part_recv[other]
    shear = shear_ref[...] + step_time * rates[0:1, :tri]
    loaded = normal_ref[...] + step_time * rates[1:2, :tri]
    distance = distance_ref[...]
    ratio = distance / slip_ref[...]
    state_next = ratio + (aging_ref[...] - ratio) * jnp.exp(-heal_time / ratio)
    state_ref[...] = state_next
    evolved = evolution_ref[...] * jnp.log(state_next / distance)
    to_smem.wait()

    take_halos(2, u_a, None)
    store = pltpu.make_async_copy(out_v, out_hbm, load_sem.at[4])
    store.start()

    lane_z = lax.broadcasted_iota(jnp.int32, (1, nz), 1)

    def answer(source, _):
        for s in range(cap):
            c = req_smem[source, 0, gx * cap + s]
            row = out_v[c // (cy * nz), pl.ds((c // nz) % cy, 1), :]
            row = jnp.where(lane_z == c % nz, row, 0.0)
            picked = row[:, :LANES]
            for j in range(1, nb):
                picked = picked + row[:, j * LANES : (j + 1) * LANES]
            ans_send[source, s : s + 1, :] = picked
        return 0

    lax.fori_loop(0, n_gx, answer, 0)

    def ans_copy(off):
        to = (gx + off) % n_gx
        return remote(
            ans_send.at[to], ans_recv.at[gx], ans_ssem.at[off], ans_rsem.at[off], to, gy
        )

    for off in range(1, n_gx):
        ans_copy(off).start()
    ans_recv[pl.ds(gx, 1)] = ans_send[pl.ds(gx, 1)]
    for off in range(1, n_gx):
        remote(
            ans_send.at[0],
            ans_recv.at[(gx + n_gx - off) % n_gx],
            ans_ssem.at[off],
            ans_rsem.at[off],
            gx,
            gy,
        ).wait_recv()
    n_slot = n_gx * cap_pad
    answers = jnp.sum(ans_recv[...].reshape(n_slot, LANES), axis=1, keepdims=True)
    mine = lax.broadcasted_iota(jnp.int32, (n_slot, tri), 0) == slot_row
    fault = jnp.sum(jnp.where(mine, answers, 0.0), axis=0, keepdims=True)
    log_ref[...] = (shear / (loaded - fault) - friction_ref - evolved) / direct_ref[...]

    for side in range(2):

        @pl.when(send_when_x[side])
        def _():
            first_x_copy(side, 0).wait_send()
            first_x_copy(side, 1).wait_send()
            later_x_copy(side, 0, u_b).wait_send()
            later_x_copy(side, 1, u_a).wait_send()

        @pl.when(send_when_y[side])
        def _():
            for turn in range(SWEEPS):
                y_copy(side, turn).wait_send()

    for g in range(n_gx):

        @pl.when((g != gx) | (slip_gy != gy))
        def _():
            slip_copy(g).wait_send()

    for off in range(1, n_gx):
        req_copy(off).wait_send()
        ans_copy(off).wait_send()
    for off in range(1, n_gy):
        part_copy(off).wait_send()
    store.wait()


def g_tile(g_in, load_g, part, comp, b, tri):
    if part == 0 and comp == 0 and b == 0:
        load_g.wait()
    return g_in[comp, part * tri : (part + 1) * tri, b * LANES : (b + 1) * LANES]


def local(
    pressure,
    permeability,
    kernel,
    slip_rate,
    aging_state,
    normal_stress,
    shear_stress,
    direct_effect,
    evolution_effect,
    slip_distance,
    tri_owner,
    tri_cell,
):
    n_gx, n_gy = lax.axis_size("gx"), lax.axis_size("gy")
    cx, cy, nz = pressure.shape
    tri = slip_rate.shape[0]
    _, rows, cols = kernel.shape
    cap = max(2, 2 * tri // n_gx)
    cap_pad = -(-cap // 8) * 8
    nb = nz // LANES
    yp = cy + 8
    padded = ((cx + 2) * nb * yp + 8, LANES)
    dense = (cx * nb * cy, LANES)
    width = -(-n_gx * cap // LANES) * LANES
    dims = (n_gx, n_gy, cx, cy, nz, tri, rows, cols, cap, cap_pad)
    f32, i32 = jnp.float32, jnp.int32
    dma = pltpu.SemaphoreType.DMA
    vec = lambda a: a.reshape(1, tri)
    any_spec = pl.BlockSpec(memory_space=pl.ANY)
    vmem_spec = pl.BlockSpec(memory_space=pltpu.VMEM)
    out, state, log = pl.pallas_call(
        functools.partial(step_kernel, dims),
        out_shape=(
            jax.ShapeDtypeStruct(pressure.shape, f32),
            jax.ShapeDtypeStruct((1, tri), f32),
            jax.ShapeDtypeStruct((1, tri), f32),
        ),
        in_specs=[any_spec] * 3 + [vmem_spec] * 9,
        out_specs=(any_spec, vmem_spec, vmem_spec),
        scratch_shapes=[
            pltpu.VMEM(pressure.shape, f32),
            pltpu.VMEM(pressure.shape, f32),
            pltpu.VMEM(kernel.shape, f32),
            pltpu.VMEM(pressure.shape, f32),
            pltpu.VMEM(padded, f32),
            pltpu.VMEM(padded, f32),
            pltpu.VMEM(padded, f32),
            pltpu.VMEM(dense, f32),
            pltpu.VMEM(dense, f32),
            pltpu.VMEM(dense, f32),
            pltpu.VMEM((2, 2, cy, nz), f32),
            pltpu.VMEM((SWEEPS - 1, 2, nb * yp - 8, LANES), f32),
            pltpu.VMEM((2, 2, cx * nb, LANES), f32),
            pltpu.VMEM((2, 2, cx * nb, LANES), f32),
            pltpu.VMEM((SWEEPS - 1, 2, cx * nb, LANES), f32),
            pltpu.VMEM((SWEEPS - 1, 2, cx * nb, LANES), f32),
            pltpu.VMEM((1, 1, LANES), f32),
            pltpu.VMEM((n_gx, 1, LANES), f32),
            pltpu.VMEM((1, 1, width), i32),
            pltpu.VMEM((n_gx, 1, width), i32),
            pltpu.SMEM((n_gx, 1, width), i32),
            pltpu.VMEM((n_gy, 2, LANES), f32),
            pltpu.VMEM((n_gy, 2, LANES), f32),
            pltpu.VMEM((n_gx, cap_pad, LANES), f32),
            pltpu.VMEM((n_gx, cap_pad, LANES), f32),
            dma((5,)),
            dma((2, 2)),
            dma((2, 2)),
            dma((SWEEPS - 1, 2)),
            dma((SWEEPS - 1, 2)),
            dma((SWEEPS, 2)),
            dma((SWEEPS, 2)),
            dma((n_gx,)),
            dma((n_gx,)),
            dma((n_gx,)),
            dma((n_gx,)),
            dma((n_gy,)),
            dma((n_gy,)),
            dma((n_gx,)),
            dma((n_gx,)),
        ],
        compiler_params=pltpu.CompilerParams(collective_id=0, has_side_effects=True),
        name="fault_step",
    )(
        pressure,
        permeability,
        kernel,
        vec(slip_rate),
        vec(aging_state),
        vec(normal_stress),
        vec(shear_stress),
        vec(direct_effect),
        vec(evolution_effect),
        vec(slip_distance),
        vec(tri_owner),
        vec(tri_cell),
    )
    return out, state.reshape(tri), log.reshape(tri)


def solution(mesh):
    fault = P(("gx", "gy"))
    field = P("gx", "gy", None)
    in_specs = (field, field, P(None, "gx", "gy")) + (fault,) * 7 + (P(("gx", "gy"), None), fault)
    out_specs = (field, fault, fault)
    return jax.shard_map(local, mesh=mesh, in_specs=in_specs, out_specs=out_specs, check_vma=False)
```

```python
import functools

import jax
import jax.numpy as jnp
from jax import lax
from jax.experimental import pallas as pl
from jax.experimental.pallas import tpu as pltpu
from jax.sharding import PartitionSpec as P

SWEEPS = 3
LANES = 128
MESH = pl.DeviceIdType.MESH

conductance = 0.15
step_time = 1.0
heal_time = 0.5
friction_ref = 0.6


def step_kernel(
    dims,
    p_hbm,
    k_hbm,
    g_hbm,
    slip_ref,
    aging_ref,
    normal_ref,
    shear_ref,
    direct_ref,
    evolution_ref,
    distance_ref,
    owner_ref,
    cell_ref,
    out_hbm,
    state_ref,
    log_ref,
    p_in,
    k_in,
    g_in,
    out_v,
    root,
    u_a,
    u_b,
    coef_a,
    coef_c,
    inv,
    first_x,
    later_x,
    first_y_send,
    first_y,
    later_y_send,
    later_y,
    slip_send,
    slip_recv,
    req_send,
    req_recv,
    req_smem,
    part_send,
    part_recv,
    ans_send,
    ans_recv,
    load_sem,
    fx_send,
    fx_recv,
    lx_send,
    lx_recv,
    y_send,
    y_recv,
    slip_ssem,
    slip_rsem,
    req_ssem,
    req_rsem,
    part_ssem,
    part_rsem,
    ans_ssem,
    ans_rsem,
):
    n_gx, n_gy, cx, cy, nz, tri, rows, cols, cap, cap_pad = dims
    nb = nz // LANES
    yp = cy + 8
    gx, gy = lax.axis_index("gx"), lax.axis_index("gy")
    dev = gx * n_gy + gy
    slip_gy = dev // n_gx
    slip_slot = dev % n_gx
    lane = lax.broadcasted_iota(jnp.int32, (1, LANES), 1)

    load_k = pltpu.make_async_copy(k_hbm, k_in, load_sem.at[0])
    load_p = pltpu.make_async_copy(p_hbm, p_in, load_sem.at[1])
    load_g = pltpu.make_async_copy(g_hbm, g_in, load_sem.at[2])
    load_k.start()
    load_p.start()
    load_g.start()

    barrier = pltpu.get_barrier_semaphore()

    def greet(x, y):
        pl.semaphore_signal(barrier, inc=1, device_id={"gx": x, "gy": y}, device_id_type=MESH)

    for off in range(1, n_gx):
        greet((gx + off) % n_gx, gy)
    for off in range(1, n_gy):
        greet(gx, (gy + off) % n_gy)
    for i in range(n_gx):
        source = gy * n_gx + i

        @pl.when(source != dev)
        def _():
            greet(source // n_gy, source % n_gy)

    zero = jnp.zeros((8, LANES), jnp.float32)
    n_col = (cx + 2) * nb
    for ref in (root, u_a, u_b):

        def clear_pad(c, _, ref=ref):
            ref[pl.ds(pl.multiple_of(c * yp, 8), 8), :] = zero
            return 0

        lax.fori_loop(0, n_col + 1, clear_pad, 0)

        def clear_end(c, _, ref=ref):
            ref[pl.ds(pl.multiple_of(c * 8, 8), 8), :] = zero
            ref[pl.ds(pl.multiple_of((cx + 1) * nb * yp + c * 8, 8), 8), :] = zero
            return 0

        lax.fori_loop(0, nb * yp // 8, clear_end, 0)

    slip_send[...] = jnp.zeros_like(slip_send)
    slip_send[0, :, :tri] = slip_ref[...]

    owner_row = owner_ref[...]
    cell_row = cell_ref[...]
    t_row = lax.broadcasted_iota(jnp.int32, (tri, tri), 1)
    t_col = lax.broadcasted_iota(jnp.int32, (tri, tri), 0)
    eye = t_row == t_col
    owner_wide = jnp.broadcast_to(owner_row, (tri, tri))
    owner_col = jnp.sum(jnp.where(eye, owner_wide, 0), axis=1, keepdims=True)
    cell_col = jnp.sum(
        jnp.where(eye, jnp.broadcast_to(cell_row, (tri, tri)), 0), axis=1, keepdims=True
    )
    same = owner_col == owner_wide
    one_below = jnp.where(same & (t_row < t_col), 1, 0)
    one_above = jnp.where(same & (t_col < t_row), 1, 0)
    rank_col = jnp.sum(one_below, axis=1, keepdims=True)
    rank_row = jnp.sum(one_above, axis=0, keepdims=True)
    slot_col = owner_col * cap + rank_col
    slot_row = owner_row * cap_pad + rank_row
    width = req_send.shape[-1]
    slot_lane = lax.broadcasted_iota(jnp.int32, (tri, width), 1)
    req_send[0] = jnp.sum(jnp.where(slot_col == slot_lane, cell_col, 0), axis=0, keepdims=True)
    req_recv[pl.ds(gx, 1)] = req_send[...]

    @pl.when(slip_gy == gy)
    def _():
        slip_recv[pl.ds(slip_slot, 1)] = slip_send[...]

    alone = jnp.where(slip_gy == gy, 1, 0)
    pl.semaphore_wait(barrier, n_gx - 1 + n_gy - 1 + n_gx - alone)

    def remote(src, dst, send, recv, x, y):
        return pltpu.make_async_remote_copy(
            src_ref=src,
            dst_ref=dst,
            send_sem=send,
            recv_sem=recv,
            device_id={"gx": x, "gy": y},
            device_id_type=MESH,
        )

    has_lo_x, has_hi_x = gx > 0, gx < n_gx - 1
    has_lo_y, has_hi_y = gy > 0, gy < n_gy - 1
    lo_x, hi_x = jnp.maximum(gx - 1, 0), jnp.minimum(gx + 1, n_gx - 1)
    lo_y, hi_y = jnp.maximum(gy - 1, 0), jnp.minimum(gy + 1, n_gy - 1)

    def first_x_copy(side, which):
        src = (k_hbm, p_hbm)[which].at[cx - 1 if side == 0 else 0]
        return remote(
            src,
            first_x.at[side, which],
            fx_send.at[side, which],
            fx_recv.at[side, which],
            hi_x if side == 0 else lo_x,
            gy,
        )

    def later_x_copy(side, turn, ref):
        plane = cx if side == 0 else 1
        src = ref.at[pl.ds(plane * nb * yp + 8, nb * yp - 8), :]
        return remote(
            src,
            later_x.at[turn, side],
            lx_send.at[turn, side],
            lx_recv.at[turn, side],
            hi_x if side == 0 else lo_x,
            gy,
        )

    def y_copy(side, turn):
        if turn == 0:
            src, dst = first_y_send.at[side], first_y.at[side]
        else:
            src, dst = later_y_send.at[turn - 1, side], later_y.at[turn - 1, side]
        return remote(
            src,
            dst,
            y_send.at[turn, side],
            y_recv.at[turn, side],
            gx,
            hi_y if side == 0 else lo_y,
        )

    send_when_x = (has_hi_x, has_lo_x)
    recv_when_x = (has_lo_x, has_hi_x)
    send_when_y = (has_hi_y, has_lo_y)
    recv_when_y = (has_lo_y, has_hi_y)

    for side in range(2):

        @pl.when(send_when_x[side])
        def _():
            first_x_copy(side, 0).start()
            first_x_copy(side, 1).start()

    def req_copy(off):
        return remote(
            req_send.at[0],
            req_recv.at[gx],
            req_ssem.at[off],
            req_rsem.at[off],
            (gx + off) % n_gx,
            gy,
        )

    def slip_copy(g):
        return remote(
            slip_send.at[0],
            slip_recv.at[slip_slot],
            slip_ssem.at[g],
            slip_rsem.at[slip_slot],
            g,
            slip_gy,
        )

    for g in range(n_gx):

        @pl.when((g != gx) | (slip_gy != gy))
        def _():
            slip_copy(g).start()

    for off in range(1, n_gx):
        req_copy(off).start()

    load_k.wait()
    load_p.wait()

    def prepare(x, _):
        for j in range(nb):
            k = k_in[x, :, j * LANES : (j + 1) * LANES]
            p = p_in[x, :, j * LANES : (j + 1) * LANES]
            r = lax.rsqrt(k)
            s = k * r
            at = pl.ds(pl.multiple_of(((x + 1) * nb + j) * yp + 8, 8), cy)
            dense = pl.ds(pl.multiple_of((x * nb + j) * cy, 8), cy)
            root[at, :] = s
            u_a[at, :] = s * p
            inv[dense, :] = r
            coef_c[dense, :] = conductance * k
        return 0

    lax.fori_loop(0, cx, prepare, 0)

    n_face = cx * nb

    def face(y):
        return pl.ds(nb * yp + 8 + y, n_face, stride=yp)

    def dense_face(y):
        return pl.ds(y, n_face, stride=cy)

    y_of = (cy - 1, 0)
    for side in range(2):
        first_y_send[side, 0] = root[face(y_of[side]), :]
        first_y_send[side, 1] = u_a[face(y_of[side]), :]
    for side in range(2):

        @pl.when(send_when_y[side])
        def _():
            y_copy(side, 0).start()

    chunk = 16

    def around(ref, x, y0):
        here, sums = [], []
        for j in range(nb):
            at = ((x + 1) * nb + j) * yp + 8 + y0
            here.append(ref[pl.ds(pl.multiple_of(at, 8), chunk), :])
        for j in range(nb):
            at = ((x + 1) * nb + j) * yp + 8 + y0
            before = here[j - 1] if j > 0 else 0.0
            after = here[j + 1] if j < nb - 1 else 0.0
            left = pltpu.roll(jnp.where(lane == LANES - 1, before, here[j]), 1, 1)
            right = pltpu.roll(jnp.where(lane == 0, after, here[j]), LANES - 1, 1)
            total = ref[pl.ds(pl.multiple_of(at + nb * yp, 8), chunk), :]
            total = total + ref[pl.ds(pl.multiple_of(at - nb * yp, 8), chunk), :]
            total = total + (ref[pl.ds(at + 1, chunk), :] + ref[pl.ds(at - 1, chunk), :])
            sums.append(total + (left + right))
        return here, sums

    def sweep(turn, src, dst):
        def plane(x, _):
            for y0 in range(0, cy, chunk):
                here, sums = around(src, x, y0)
                if turn == 0:
                    roots, root_sums = around(root, x, y0)
                for j in range(nb):
                    dense = pl.ds(pl.multiple_of((x * nb + j) * cy + y0, 8), chunk)
                    if turn == 0:
                        a = 1.0 - conductance * (roots[j] * root_sums[j])
                        coef_a[dense, :] = a
                    else:
                        a = coef_a[dense, :]
                    new = a * here[j] + coef_c[dense, :] * sums[j]
                    if turn < SWEEPS - 1:
                        at = ((x + 1) * nb + j) * yp + 8 + y0
                        dst[pl.ds(pl.multiple_of(at, 8), chunk), :] = new
                    else:
                        out_v[x, y0 : y0 + chunk, j * LANES : (j + 1) * LANES] = (
                            new * inv[dense, :]
                        )
            return 0

        lax.fori_loop(0, cx, plane, 0)

    def fix_x(turn, side, src, dst):
        x = 0 if side == 0 else cx - 1
        for j in range(nb):
            at = pl.ds(((x + 1) * nb + j) * yp + 8, cy)
            dense = pl.ds((x * nb + j) * cy, cy)
            if turn == 0:
                k = first_x[side, 0, :, j * LANES : (j + 1) * LANES]
                s = k * lax.rsqrt(k)
                halo = s * first_x[side, 1, :, j * LANES : (j + 1) * LANES]
                less = conductance * (root[at, :] * s)
                coef_a[dense, :] = coef_a[dense, :] - less
                dst[at, :] = dst[at, :] + (coef_c[dense, :] * halo - less * src[at, :])
            else:
                halo = later_x[turn - 1, side, pl.ds(j * yp, cy), :]
                if turn < SWEEPS - 1:
                    dst[at, :] = dst[at, :] + coef_c[dense, :] * halo
                else:
                    cols_j = slice(j * LANES, (j + 1) * LANES)
                    out_v[x, :, cols_j] = out_v[x, :, cols_j] + coef_c[dense, :] * inv[
                        dense, :
                    ] * halo

    def fix_y(turn, side, src, dst):
        y = 0 if side == 0 else cy - 1
        at, dense = face(y), dense_face(y)
        if turn == 0:
            s, halo = first_y[side, 0], first_y[side, 1]
            less = conductance * (root[at, :] * s)
            coef_a[dense, :] = coef_a[dense, :] - less
            dst[at, :] = dst[at, :] + (coef_c[dense, :] * halo - less * src[at, :])
        else:
            halo = later_y[turn - 1, side]
            if turn < SWEEPS - 1:
                dst[at, :] = dst[at, :] + coef_c[dense, :] * halo
            else:
                later_y[turn - 1, side] = coef_c[dense, :] * inv[dense, :] * halo
                for x in range(cx):
                    for j in range(nb):
                        cols_j = slice(j * LANES, (j + 1) * LANES)
                        row = x * nb + j
                        out_v[x, y : y + 1, cols_j] = (
                            out_v[x, y : y + 1, cols_j] + later_y[turn - 1, side, row : row + 1, :]
                        )

    def take_halos(turn, src, dst):
        for side in range(2):

            @pl.when(recv_when_y[side])
            def _():
                y_copy(side, turn).wait_recv()
                fix_y(turn, side, src, dst)

        for side in range(2):

            @pl.when(recv_when_x[side])
            def _():
                if turn == 0:
                    first_x_copy(side, 0).wait_recv()
                    first_x_copy(side, 1).wait_recv()
                else:
                    later_x_copy(side, turn - 1, src).wait_recv()
                fix_x(turn, side, src, dst)

    def send_halos(turn, ref):
        for side in range(2):
            later_y_send[turn - 1, side] = ref[face(y_of[side]), :]
        for side in range(2):

            @pl.when(send_when_x[side])
            def _():
                later_x_copy(side, turn - 1, ref).start()

        for side in range(2):

            @pl.when(send_when_y[side])
            def _():
                y_copy(side, turn).start()

    sweep(0, u_a, u_b)
    take_halos(0, u_a, u_b)
    send_halos(1, u_b)

    for i in range(n_gx):

        @pl.when(gy * n_gx + i != dev)
        def _():
            remote(
                slip_send.at[0], slip_recv.at[i], slip_ssem.at[0], slip_rsem.at[i], gx, gy
            ).wait_recv()

    n_cb = cols // LANES
    segment = [jnp.zeros((1, LANES), jnp.float32) for _ in range(n_cb)]
    for i in range(n_gx):
        first, shift = (i * tri) // LANES, (i * tri) % LANES
        row = slip_recv[i]
        if shift:
            row = pltpu.roll(row, shift, 1)
        segment[first] = segment[first] + jnp.where(lane >= shift, row, 0.0)
        if shift + tri > LANES:
            segment[first + 1] = segment[first + 1] + jnp.where(lane < shift, row, 0.0)
    eye_f = lax.broadcasted_iota(jnp.int32, (tri, LANES), 0) == lax.broadcasted_iota(
        jnp.int32, (tri, LANES), 1
    )
    for part in range(n_gy):
        for comp in range(2):
            total = jnp.zeros((tri, LANES), jnp.float32)
            for b in range(n_cb):
                block = g_tile(g_in, load_g, part, comp, b, tri)
                total = total + block * segment[b]
            sums = jnp.sum(total, axis=1, keepdims=True)
            part_send[part, comp : comp + 1, :] = jnp.sum(
                jnp.where(eye_f, sums, 0.0), axis=0, keepdims=True
            )

    def part_copy(off):
        to = (gy + off) % n_gy
        return remote(
            part_send.at[to], part_recv.at[gy], part_ssem.at[off], part_rsem.at[off], gx, to
        )

    part_recv[pl.ds(gy, 1)] = part_send[pl.ds(gy, 1)]
    for off in range(1, n_gy):
        part_copy(off).start()

    sweep(1, u_b, u_a)
    take_halos(1, u_b, u_a)
    send_halos(2, u_a)
    for off in range(1, n_gx):
        remote(
            req_send.at[0],
            req_recv.at[(gx + n_gx - off) % n_gx],
            req_ssem.at[off],
            req_rsem.at[off],
            gx,
            gy,
        ).wait_recv()
    to_smem = pltpu.make_async_copy(req_recv, req_smem, load_sem.at[3])
    to_smem.start()
    ans_send[...] = jnp.zeros_like(ans_send)
    sweep(2, u_a, None)

    for off in range(1, n_gy):
        remote(
            part_send.at[0],
            part_recv.at[(gy + n_gy - off) % n_gy],
            part_ssem.at[off],
            part_rsem.at[off],
            gx,
            gy,
        ).wait_recv()
    rates = part_recv[0]
    for other in range(1, n_gy):
        rates = rates + part_recv[other]
    shear = shear_ref[...] + step_time * rates[0:1, :tri]
    loaded = normal_ref[...] + step_time * rates[1:2, :tri]
    distance = distance_ref[...]
    ratio = distance / slip_ref[...]
    state_next = ratio + (aging_ref[...] - ratio) * jnp.exp(-heal_time / ratio)
    state_ref[...] = state_next
    evolved = evolution_ref[...] * jnp.log(state_next / distance)
    to_smem.wait()

    take_halos(2, u_a, None)
    store = pltpu.make_async_copy(out_v, out_hbm, load_sem.at[4])
    store.start()

    lane_z = lax.broadcasted_iota(jnp.int32, (1, nz), 1)

    def answer(source, _):
        for s in range(cap):
            c = req_smem[source, 0, gx * cap + s]
            row = out_v[part_of(c, cy * nz), pl.ds(rest_of(part_of(c, nz), cy), 1), :]
            row = jnp.where(lane_z == rest_of(c, nz), row, 0.0)
            picked = row[:, :LANES]
            for j in range(1, nb):
                picked = picked + row[:, j * LANES : (j + 1) * LANES]
            ans_send[source, s : s + 1, :] = picked
        return 0

    lax.fori_loop(0, n_gx, answer, 0)

    def ans_copy(off):
        to = (gx + off) % n_gx
        return remote(
            ans_send.at[to], ans_recv.at[gx], ans_ssem.at[off], ans_rsem.at[off], to, gy
        )

    for off in range(1, n_gx):
        ans_copy(off).start()
    ans_recv[pl.ds(gx, 1)] = ans_send[pl.ds(gx, 1)]
    for off in range(1, n_gx):
        remote(
            ans_send.at[0],
            ans_recv.at[(gx + n_gx - off) % n_gx],
            ans_ssem.at[off],
            ans_rsem.at[off],
            gx,
            gy,
        ).wait_recv()
    n_slot = n_gx * cap_pad
    answers = jnp.sum(ans_recv[...].reshape(n_slot, LANES), axis=1, keepdims=True)
    mine = lax.broadcasted_iota(jnp.int32, (n_slot, tri), 0) == slot_row
    fault = jnp.sum(jnp.where(mine, answers, 0.0), axis=0, keepdims=True)
    log_ref[...] = (shear / (loaded - fault) - friction_ref - evolved) / direct_ref[...]

    for side in range(2):

        @pl.when(send_when_x[side])
        def _():
            first_x_copy(side, 0).wait_send()
            first_x_copy(side, 1).wait_send()
            later_x_copy(side, 0, u_b).wait_send()
            later_x_copy(side, 1, u_a).wait_send()

        @pl.when(send_when_y[side])
        def _():
            for turn in range(SWEEPS):
                y_copy(side, turn).wait_send()

    for g in range(n_gx):

        @pl.when((g != gx) | (slip_gy != gy))
        def _():
            slip_copy(g).wait_send()

    for off in range(1, n_gx):
        req_copy(off).wait_send()
        ans_copy(off).wait_send()
    for off in range(1, n_gy):
        part_copy(off).wait_send()
    store.wait()


def part_of(value, size):
    if size & (size - 1) == 0:
        return lax.shift_right_logical(value, jnp.int32(size.bit_length() - 1))
    return lax.div(value, jnp.int32(size))


def rest_of(value, size):
    if size & (size - 1) == 0:
        return value & (size - 1)
    return lax.rem(value, jnp.int32(size))


def copy_kernel(p_hbm, state_in, log_in, out_hbm, state_ref, log_ref, buf, in_sem, out_sem):
    planes = p_hbm.shape[0]
    n = in_sem.shape[0]
    reads, writes = [], []
    for i in range(n):
        part = pl.ds(i * planes // n, planes // n)
        reads.append(pltpu.make_async_copy(p_hbm.at[part], buf.at[part], in_sem.at[i]))
        writes.append(pltpu.make_async_copy(buf.at[part], out_hbm.at[part], out_sem.at[i]))
        reads[-1].start()
    state_ref[...] = state_in[...]
    log_ref[...] = log_in[...]
    for i in range(n):
        reads[i].wait()
        writes[i].start()
    for i in range(n):
        writes[i].wait()


def g_tile(g_in, load_g, part, comp, b, tri):
    if part == 0 and comp == 0 and b == 0:
        load_g.wait()
    return g_in[comp, part * tri : (part + 1) * tri, b * LANES : (b + 1) * LANES]


def local(
    pressure,
    permeability,
    kernel,
    slip_rate,
    aging_state,
    normal_stress,
    shear_stress,
    direct_effect,
    evolution_effect,
    slip_distance,
    tri_owner,
    tri_cell,
):
    n_gx, n_gy = lax.axis_size("gx"), lax.axis_size("gy")
    cx, cy, nz = pressure.shape
    tri = slip_rate.shape[0]
    _, rows, cols = kernel.shape
    cap = max(2, 2 * tri // n_gx)
    cap_pad = -(-cap // 8) * 8
    nb = nz // LANES
    yp = cy + 8
    padded = ((cx + 2) * nb * yp + 8, LANES)
    dense = (cx * nb * cy, LANES)
    width = -(-n_gx * cap // LANES) * LANES
    dims = (n_gx, n_gy, cx, cy, nz, tri, rows, cols, cap, cap_pad)
    f32, i32 = jnp.float32, jnp.int32
    dma = pltpu.SemaphoreType.DMA
    vec = lambda a: a.reshape(1, tri)
    any_spec = pl.BlockSpec(memory_space=pl.ANY)
    vmem_spec = pl.BlockSpec(memory_space=pltpu.VMEM)
    out, state, log = pl.pallas_call(
        functools.partial(step_kernel, dims),
        out_shape=(
            jax.ShapeDtypeStruct(pressure.shape, f32),
            jax.ShapeDtypeStruct((1, tri), f32),
            jax.ShapeDtypeStruct((1, tri), f32),
        ),
        in_specs=[any_spec] * 3 + [vmem_spec] * 9,
        out_specs=(any_spec, vmem_spec, vmem_spec),
        scratch_shapes=[
            pltpu.VMEM(pressure.shape, f32),
            pltpu.VMEM(pressure.shape, f32),
            pltpu.VMEM(kernel.shape, f32),
            pltpu.VMEM(pressure.shape, f32),
            pltpu.VMEM(padded, f32),
            pltpu.VMEM(padded, f32),
            pltpu.VMEM(padded, f32),
            pltpu.VMEM(dense, f32),
            pltpu.VMEM(dense, f32),
            pltpu.VMEM(dense, f32),
            pltpu.VMEM((2, 2, cy, nz), f32),
            pltpu.VMEM((SWEEPS - 1, 2, nb * yp - 8, LANES), f32),
            pltpu.VMEM((2, 2, cx * nb, LANES), f32),
            pltpu.VMEM((2, 2, cx * nb, LANES), f32),
            pltpu.VMEM((SWEEPS - 1, 2, cx * nb, LANES), f32),
            pltpu.VMEM((SWEEPS - 1, 2, cx * nb, LANES), f32),
            pltpu.VMEM((1, 1, LANES), f32),
            pltpu.VMEM((n_gx, 1, LANES), f32),
            pltpu.VMEM((1, 1, width), i32),
            pltpu.VMEM((n_gx, 1, width), i32),
            pltpu.SMEM((n_gx, 1, width), i32),
            pltpu.VMEM((n_gy, 2, LANES), f32),
            pltpu.VMEM((n_gy, 2, LANES), f32),
            pltpu.VMEM((n_gx, cap_pad, LANES), f32),
            pltpu.VMEM((n_gx, cap_pad, LANES), f32),
            dma((5,)),
            dma((2, 2)),
            dma((2, 2)),
            dma((SWEEPS - 1, 2)),
            dma((SWEEPS - 1, 2)),
            dma((SWEEPS, 2)),
            dma((SWEEPS, 2)),
            dma((n_gx,)),
            dma((n_gx,)),
            dma((n_gx,)),
            dma((n_gx,)),
            dma((n_gy,)),
            dma((n_gy,)),
            dma((n_gx,)),
            dma((n_gx,)),
        ],
        compiler_params=pltpu.CompilerParams(collective_id=0, has_side_effects=True),
        name="fault_step",
    )(
        pressure,
        permeability,
        kernel,
        vec(slip_rate),
        vec(aging_state),
        vec(normal_stress),
        vec(shear_stress),
        vec(direct_effect),
        vec(evolution_effect),
        vec(slip_distance),
        vec(tri_owner),
        vec(tri_cell),
    )
    pieces = cx if cx < 8 else 8 if cx % 8 == 0 else 1
    out, state, log = pl.pallas_call(
        copy_kernel,
        out_shape=(
            jax.ShapeDtypeStruct(pressure.shape, f32),
            jax.ShapeDtypeStruct((1, tri), f32),
            jax.ShapeDtypeStruct((1, tri), f32),
        ),
        in_specs=[any_spec, vmem_spec, vmem_spec],
        out_specs=(any_spec, vmem_spec, vmem_spec),
        scratch_shapes=[pltpu.VMEM(pressure.shape, f32), dma((pieces,)), dma((pieces,))],
        name="write_out",
    )(out, state, log)
    return out, state.reshape(tri), log.reshape(tri)


def solution(mesh):
    fault = P(("gx", "gy"))
    field = P("gx", "gy", None)
    in_specs = (field, field, P(None, "gx", "gy")) + (fault,) * 7 + (P(("gx", "gy"), None), fault)
    out_specs = (field, fault, fault)
    return jax.shard_map(local, mesh=mesh, in_specs=in_specs, out_specs=out_specs, check_vma=False)
```
